32 devices in a mesh: dp: 4 (over y, x), section: 4 (over z), mp: 2 (over core).
Axes of the slice: x: 2, y: 2, z: 4, core: 2. Of those that a mesh axis runs over, the one named last changes fastest.
Arguments:
- enc_rows: bfloat16 [4, 1024, 4096], P('dp', ('section', 'mp')), may hold values from -6 to 6
- pack_index: int32 [4, 1024], P('dp'), may hold values from 0 to 1023, each once within a row
- enc_segments: int32 [4, 1024], P('dp'), may hold values from 0 to 3, never falling along the last dimension, each value on 1 to 512 neighbouring positions
- dec_segments: int32 [4, 256], P('dp'), may hold values from 0 to 3, never falling along the last dimension, each value on 1 to 128 neighbouring positions
- dec_inputs: bfloat16 [4, 4, 256, 4096], P('dp', 'section', 'mp'), may hold values from -6 to 6
- norm_gain: bfloat16 [4, 4096], P('section'), may hold values from 0.099609375 to 1.8984375
- w_query: bfloat16 [4, 4096, 2048], P('section', None, 'mp'), may hold values from -0.09375 to 0.09375
- w_key: bfloat16 [4, 4096, 2048], P('section', None, 'mp'), may hold values from -0.09375 to 0.09375
- w_value: bfloat16 [4, 4096, 2048], P('section', None, 'mp'), may hold values from -0.09375 to 0.09375
- w_out: bfloat16 [4, 2048, 4096], P('section', 'mp'), may hold values from -0.125 to 0.125
- cotangent: bfloat16 [4, 256, 4096], P('dp', 'mp'), may hold values from -6 to 6
Outputs:
- dec_grads: bfloat16 [4, 4, 256, 4096], P('dp', 'section', 'mp')
- enc_grads: float32 [4, 1024, 4096], P('dp', ('section', 'mp'))
The draws below stay inside these ranges and needn't reach their ends.
Inputs may be any that keep to these rules, and one draw needn't show every extreme that they name: `dec_segments`: every sequence id of a group occurs among both its decoder tokens and its packed encoder positions.
All inputs are finite; a program needn't handle non-finite values.
Results may differ from the reference program's by a relative error of at most 0.024.
Values may be sent and summed in bfloat16 or wider, within the bound.
No kernel may reach another device: no remote copies, remote signals or barrier semaphores. Data moves between devices by JAX's collectives and lax.ppermute only.
A program may use at most 192 MiB of HBM per device.

```python
import math
import jax
import jax.numpy as jnp
import numpy as np
from jax import lax

D = 4096
HEADS = 32
HD = 64
TQ = 256
E = 1024
NSEG = 4
LAYERS = 4
GROUPS = 4
N_MP = 2


def block_scale(key, extent, split, least, top_value):
    def one(position, shards_of):
        heights = jax.random.uniform(jax.random.fold_in(jax.random.fold_in(key, 6), position), (shards_of,), jnp.float32, least / len(split), top_value / len(split))
        return jnp.repeat(jnp.exp(heights), extent[position] // shards_of).reshape((-1,) + (1,) * (len(extent) - position - 1))

    level = one(*split[0])
    for cut in split[1:]:
        level = level * one(*cut)
    return level


def split_up(count, total, limit, slope):
    portions = [(1 << 20) // math.isqrt(rank ** slope) + 1 for rank in range(2, count + 1)]
    surplus, counts = total - limit - (count - 1), [1] * (count - 1)
    while surplus > 0:
        movable = [i for i in range(count - 1) if counts[i] < limit]
        mass, left = sum([portions[i] for i in movable]), surplus
        for i in movable:
            more = min(limit - counts[i], max(1, left * portions[i] // mass), surplus)
            counts[i] = counts[i] + more
            surplus = surplus - more
    return np.array([limit] + counts)


def uneven(key, amount, total, reach, skew):
    if amount == 2:
        one = jax.random.randint(key, (), max(1, total - reach), min(reach, total - 1) + 1)
        return jnp.stack([one, total - one])
    lengths = jnp.asarray(split_up(amount, total, reach, skew), jnp.int32)
    twos = (amount - 1) // 2
    source_of, taker = lengths[1:1 + 2 * twos:2], lengths[2:2 + 2 * twos:2]
    room = jnp.minimum(source_of - 1, reach - taker)
    passed = jax.random.randint(jax.random.fold_in(key, 1), (twos,), 0, 1 << 20) % (room + 1)
    lengths = lengths.at[1:1 + 2 * twos:2].set(source_of - passed).at[2:2 + 2 * twos:2].set(taker + passed)
    return lengths[jax.random.permutation(jax.random.fold_in(key, 2), amount)]


def scatter_about(own_key, extent, scale, reach, cuts=(), dtype=jnp.bfloat16):
    loudness = block_scale(own_key, extent, cuts, -0.22, 0.18) if cuts else 1.0
    values = jax.random.normal(own_key, extent, jnp.float32) * scale * loudness
    return jnp.minimum(jnp.maximum(values, -reach), reach).astype(dtype)


def setup_inputs(seed: int = 0) -> dict:
    key_list = jax.random.split(jax.random.key(seed), 12)
    return {
        "enc_rows": scatter_about(key_list[0], (GROUPS, E, D), 1.0, 6.0, ((0, 4), (1, 8))),
        "pack_index": jax.vmap(lambda own: jax.random.permutation(own, E))(jax.random.split(key_list[1], GROUPS)).reshape((GROUPS, E)).astype(jnp.int32),
        "enc_segments": jax.vmap(lambda own: jnp.searchsorted(jnp.cumsum(uneven(own, NSEG, E, E // 2, 2)), jnp.arange(E), side="right"))(jax.random.split(key_list[2], GROUPS)).reshape((GROUPS, E)).astype(jnp.int32),
        "dec_segments": jax.vmap(lambda own: jnp.searchsorted(jnp.cumsum(uneven(own, NSEG, TQ, TQ // 2, 2)), jnp.arange(TQ), side="right"))(jax.random.split(key_list[3], GROUPS)).reshape((GROUPS, TQ)).astype(jnp.int32),
        "dec_inputs": scatter_about(key_list[4], (GROUPS, LAYERS, TQ, D), 1.0, 6.0, ((0, 4), (1, 4), (2, 2))),
        "norm_gain": jnp.clip(1.0 + 0.18 * jax.random.normal(key_list[5], (LAYERS, D), jnp.float32), 0.099609375, 1.8984375).astype(jnp.bfloat16),
        "w_query": scatter_about(key_list[6], (LAYERS, D, HEADS * HD), D ** -0.5, 0.09375, ((0, 4), (2, 2))),
        "w_key": scatter_about(key_list[7], (LAYERS, D, HEADS * HD), D ** -0.5, 0.09375, ((0, 4), (2, 2))),
        "w_value": scatter_about(key_list[8], (LAYERS, D, HEADS * HD), D ** -0.5, 0.09375, ((0, 4), (2, 2))),
        "w_out": scatter_about(key_list[9], (LAYERS, HEADS * HD, D), (HEADS * HD) ** -0.5, 0.125, ((0, 4), (1, 2))),
        "cotangent": scatter_about(key_list[10], (GROUPS, TQ, D), 1.0, 6.0, ((0, 4), (1, 2))),
    }


epsilon = 1e-06
masked_value = -1e+30

def reference(enc_rows, pack_index, enc_segments, dec_segments, dec_inputs, norm_gain, w_query, w_key, w_value, w_out, cotangent):
    layer_count = w_query.shape[0]
    width = HEADS * HD
    scale_factor = HD ** (-0.5)
    token_count = dec_inputs.shape[2]
    enc_count = enc_rows.shape[1]
    dec_list = []
    enc_list = []
    for group_index in range(GROUPS):
        packing = pack_index[group_index].astype(jnp.int32)
        packed = jnp.take(enc_rows[group_index], packing, axis=0)
        allowed = dec_segments[group_index][:, None] == enc_segments[group_index][None, :]
        upstream = cotangent[group_index]
        enc_grad = jnp.zeros((enc_count, D), jnp.float32)
        layer_grads = [None] * layer_count
        for layer in reversed(range(layer_count)):
            inputs = dec_inputs[group_index, layer].astype(jnp.float32)
            recip = lax.rsqrt(lax.optimization_barrier(jnp.mean(inputs * inputs, axis=-1, keepdims=True)) + epsilon)
            unit = inputs * recip
            norm_scale = norm_gain[layer].astype(jnp.float32)
            normed = (unit * norm_scale).astype(jnp.bfloat16)
            queries = jnp.dot(normed, w_query[layer], preferred_element_type=jnp.float32).astype(jnp.bfloat16)
            key_rows = jnp.dot(packed, w_key[layer], preferred_element_type=jnp.float32).astype(jnp.bfloat16)
            value_rows = jnp.dot(packed, w_value[layer], preferred_element_type=jnp.float32).astype(jnp.bfloat16)
            query_heads = queries.astype(jnp.float32).reshape(token_count, HEADS, HD)
            key_heads = key_rows.astype(jnp.float32).reshape(enc_count, HEADS, HD)
            value_heads = value_rows.astype(jnp.float32).reshape(enc_count, HEADS, HD)
            scores = jnp.einsum('qhd,khd->hqk', query_heads, key_heads) * scale_factor
            scores = jnp.where(allowed[None], scores, masked_value)
            probs = jax.nn.softmax(scores, axis=-1)
            probs_low = probs.astype(jnp.bfloat16)
            attn_grad = jnp.dot(upstream, w_out[layer].T, preferred_element_type=jnp.float32).astype(jnp.bfloat16)
            grad_heads = attn_grad.astype(jnp.float32).reshape(token_count, HEADS, HD)
            prob_grad = jnp.einsum('qhd,khd->hqk', grad_heads, value_heads)
            score_grad = (probs * (prob_grad - lax.optimization_barrier(jnp.sum(prob_grad * probs, axis=-1, keepdims=True))) * scale_factor).astype(jnp.bfloat16)
            score_wide = score_grad.astype(jnp.float32)
            query_grad = jnp.einsum('hqk,khd->qhd', score_wide, key_heads).astype(jnp.bfloat16).reshape(token_count, width)
            key_grad = jnp.einsum('hqk,qhd->khd', score_wide, query_heads).astype(jnp.bfloat16).reshape(enc_count, width)
            value_grad = jnp.einsum('hqk,qhd->khd', probs_low.astype(jnp.float32), grad_heads).astype(jnp.bfloat16).reshape(enc_count, width)
            enc_grad = enc_grad + jnp.dot(key_grad, w_key[layer].T, preferred_element_type=jnp.float32)
            enc_grad = enc_grad + jnp.dot(value_grad, w_value[layer].T, preferred_element_type=jnp.float32)
            grouped_grad = query_grad.astype(jnp.float32).reshape(token_count, N_MP, width // N_MP)
            grouped_weight = w_query[layer].astype(jnp.float32).reshape(D, N_MP, width // N_MP)
            group_terms = jnp.einsum('qgc,dgc->gqd', grouped_grad, grouped_weight).astype(jnp.bfloat16)
            group_terms = lax.optimization_barrier(group_terms)
            norm_grad = lax.optimization_barrier(jnp.sum(group_terms.astype(jnp.float32), axis=0))
            scaled = norm_grad * norm_scale
            result = upstream.astype(jnp.float32) + recip * (scaled - unit * lax.optimization_barrier(jnp.mean(scaled * unit, axis=-1, keepdims=True)))
            result = result.astype(jnp.bfloat16)
            layer_grads[layer] = result
            upstream = result
        dec_list.append(jnp.stack(layer_grads, axis=0))
        enc_list.append(jnp.zeros((enc_count, D), jnp.float32).at[packing].set(enc_grad))
    return (jnp.stack(dec_list, axis=0), jnp.stack(enc_list, axis=0))
```

```python
import functools

import jax
import jax.numpy as jnp
from jax import lax
from jax.experimental import pallas as pl
from jax.experimental.pallas import tpu as pltpu
from jax.sharding import PartitionSpec as P

HD = 64
PAIR = 2 * HD
MICRO = 4
SKEW = 2
PIECES = 2
BLOCK = 512
OUT_BLOCK = 512
SLOTS = ((0, 1, 2, 3), (1, 2, 1, 2), (2, 3, 0, 1), (3, 0, 3, 0))

epsilon = 1e-06
masked_value = -1e30
f32 = jnp.float32
bf16 = jnp.bfloat16
NT = (((1,), (1,)), ((), ()))
NN = (((1,), (0,)), ((), ()))


def dot(a, b, dims):
    return lax.dot_general(a, b, dims, preferred_element_type=f32)


def stacked(x):
    lane = lax.broadcasted_iota(jnp.int32, x.shape, 1)
    zero = jnp.zeros_like(x)
    return jnp.concatenate(
        [jnp.where(lane < HD, x, zero), jnp.where(lane >= HD, x, zero)], axis=0
    )


def probs_kernel(q_ref, k_ref, tok_ref, key_ref, p_ref):
    q = stacked(q_ref[...].astype(f32) * (HD**-0.5)).astype(bf16)
    s = dot(q, k_ref[...], NT)
    s = jnp.where(tok_ref[0] == key_ref[...], s, masked_value)
    e = jnp.exp(s - jnp.max(s, axis=-1, keepdims=True))
    total = jnp.sum(e, axis=-1, keepdims=True)
    p_ref[0, 0] = (e * (1.0 / total)).astype(bf16)


def load_kernel(count, *refs):
    sems = refs[-1]
    copies = [
        pltpu.make_async_copy(refs[i], refs[count + i], sems.at[i]) for i in range(count)
    ]
    for copy in copies:
        copy.start()
    for copy in copies:
        copy.wait()


def project_kernel(count, *refs):
    x_refs = refs[:count]
    wk_ref, wv_ref = refs[count : count + 2]
    k_ref, v_ref, x_all = refs[-3:]

    @pl.when(pl.program_id(0) == 0)
    def _():
        start = 0
        for x in x_refs:
            x_all[start : start + x.shape[0]] = x[...]
            start += x.shape[0]

    block = k_ref.shape[1]
    cols = pl.ds(pl.multiple_of(pl.program_id(0) * block, block), block)
    k_ref[...] = dot(x_all[...], wk_ref[:, cols], NN).astype(bf16)
    v_ref[...] = dot(x_all[...], wv_ref[:, cols], NN).astype(bf16)


def back_kernel(kg_ref, vg_ref, wk_ref, wv_ref, own_ref, other_ref):
    block = own_ref.shape[1]
    place = pl.ds(pl.multiple_of(pl.program_id(0) * block, block), block)
    out = dot(kg_ref[...], wk_ref[place, :], NT) + dot(vg_ref[...], wv_ref[place, :], NT)
    rows = own_ref.shape[0]
    own_ref[...] = out[:rows].astype(bf16)
    other_ref[...] = out[rows:].astype(bf16)


def turn_kernel(parts, own_rows, slots, *refs):
    del slots
    up_refs = refs[:parts]
    wo_ref, wq_ref, k_ref, v_ref, p_ref = refs[parts : parts + 5]
    own_ref, other_ref, ds_ref, ag_ref, acc_ref = refs[-5:]
    step = pl.program_id(0)
    block = ag_ref.shape[2]
    start = pl.multiple_of(step * block, block)
    up = up_refs[0][...] if parts == 1 else jnp.concatenate([r[...] for r in up_refs], axis=0)
    rows = up.shape[0]
    grads = dot(up, wo_ref[pl.ds(start, block), :], NT).astype(bf16)
    ag_ref[0] = grads
    wide = grads.astype(f32)
    lane = lax.broadcasted_iota(jnp.int32, (rows, PAIR), 1)
    pieces = []
    for pair in range(grads.shape[1] // PAIR):
        cols = pl.ds(pl.multiple_of(start + pair * PAIR, PAIR), PAIR)
        here = wide[:, pair * PAIR : (pair + 1) * PAIR]
        pg = dot(stacked(here).astype(bf16), v_ref[:, cols], NT)
        p = p_ref[0, pair].astype(f32)
        mean = jnp.sum(pg * p, axis=-1, keepdims=True)
        ds = (p * (pg - mean)).astype(bf16)
        ds_ref[0, pair] = ds
        both = dot(ds, k_ref[:, cols], NN)
        mine = jnp.where(lane < HD, both[:rows], both[rows:]) * (HD**-0.5)
        pieces.append(mine.astype(bf16))
    qg = pieces[0] if len(pieces) == 1 else jnp.concatenate(pieces, axis=1)
    partial = dot(qg, wq_ref[:, pl.ds(start, block)], NT)

    @pl.when(step == 0)
    def _():
        acc_ref[...] = partial

    @pl.when(step > 0)
    def _():
        acc_ref[...] += partial

    @pl.when(step == pl.num_programs(0) - 1)
    def _():
        own_ref[...] = acc_ref[:own_rows].astype(bf16)
        other_ref[...] = acc_ref[own_rows:].astype(bf16)


def norm_kernel(received, slots, *refs):
    del slots
    got_refs = refs[:received]
    own_ref, up_ref, x_ref, gain_ref = refs[received : received + 4]
    mine_ref, all_ref = refs[-2:]
    x = x_ref[...].astype(f32)
    recip = lax.rsqrt(jnp.mean(x * x, axis=-1, keepdims=True) + epsilon)
    unit = x * recip
    summed = own_ref[...].astype(f32)
    for got in got_refs:
        summed = summed + got[...].astype(f32)
    scaled = summed * gain_ref[...]
    out = up_ref[...].astype(f32) + recip * (
        scaled - unit * jnp.mean(scaled * unit, axis=-1, keepdims=True)
    )
    out = out.astype(bf16)
    mine_ref[...] = out
    all_ref[...] = out


def grads_kernel(micro, ds_ref, p_ref, q_ref, ag_ref, kg_ref, vg_ref):
    rows = ag_ref.shape[1]
    enc = ds_ref.shape[-1]
    q = jnp.concatenate(
        [stacked(q_ref[i * rows : (i + 1) * rows, :].astype(f32)) for i in range(micro)], axis=0
    )
    ag = jnp.concatenate([stacked(ag_ref[i].astype(f32)) for i in range(micro)], axis=0)
    ds = ds_ref[:, 0].reshape(micro * 2 * rows, enc)
    p = p_ref[:, 0].reshape(micro * 2 * rows, enc)
    kg = dot(q.T.astype(bf16), ds, NN) * (HD**-0.5)
    vg = dot(ag.T.astype(bf16), p, NN)
    kg_ref[...] = kg.T.astype(bf16)
    vg_ref[...] = vg.T.astype(bf16)


def all_of_it(
    enc_rows,
    pack_index,
    enc_segments,
    dec_segments,
    dec_inputs,
    norm_gain,
    w_query,
    w_key,
    w_value,
    w_out,
    cotangent,
):
    wq, wk, wv, wo = w_query[0], w_key[0], w_value[0], w_out[0]
    gain = norm_gain.astype(f32)
    model, width = wq.shape
    pairs = width // PAIR
    n = lax.axis_size("mp")
    sections = lax.axis_size("section")
    me = lax.axis_index("mp")
    section = lax.axis_index("section")
    assert sections == len(SLOTS)
    share = enc_rows.shape[1]
    enc = share * n * sections
    own = dec_inputs.shape[2]
    r = own // MICRO
    m = r * n
    tokens = own * n
    params = pltpu.CompilerParams(vmem_limit_bytes=24 * 1024 * 1024)
    small = pltpu.CompilerParams(vmem_limit_bytes=14 * 1024 * 1024)

    def shifted(x, by):
        return lax.ppermute(x, "mp", [((i + by) % n, i) for i in range(n)])

    def along(x, *pairs):
        return lax.ppermute(x, "section", pairs)

    low = section < 2
    block = min(BLOCK, width)
    bp = block // PAIR
    parts = 2 if n == 2 else 1
    any_spec = pl.BlockSpec(memory_space=pl.ANY)
    resident = pl.BlockSpec(memory_space=pltpu.MemorySpace.VMEM)

    def in_hbm(x):
        return pltpu.with_memory_space_constraint(x, pltpu.MemorySpace.HBM)

    def loaded(*xs):
        return pl.pallas_call(
            functools.partial(load_kernel, len(xs)),
            in_specs=[any_spec] * len(xs),
            out_specs=[resident] * len(xs),
            out_shape=[pltpu.MemorySpace.VMEM(x.shape, x.dtype) for x in xs],
            scratch_shapes=[pltpu.SemaphoreType.DMA((len(xs),))],
            compiler_params=small,
            name="load",
        )(*map(in_hbm, xs))

    def all_parts(x):
        return [x] + [shifted(x, k) for k in range(1, n)]

    x_own = dec_inputs[0, 0]
    x_all = jnp.stack([v.reshape(MICRO, r, model) for v in all_parts(x_own)], axis=1)
    x_all = x_all.reshape(tokens, model).astype(f32)
    recip = lax.rsqrt(jnp.mean(x_all * x_all, axis=-1, keepdims=True) + epsilon)
    normed = (x_all * recip * gain).astype(bf16)
    queries = dot(normed, wq, NN).astype(bf16)
    token_ids = dec_segments[0].reshape(n, MICRO, r)
    order = jnp.remainder(me + jnp.arange(n), n)
    token_ids = jnp.take(token_ids, order, axis=0).transpose(1, 0, 2).reshape(MICRO, m)
    token_ids = jnp.concatenate([token_ids, token_ids], axis=1)[:, :, None]

    blocks = jnp.asarray(SLOTS, jnp.int32)[:, section]
    stored = (blocks[:, None] * n + order[None, :])[:, :, None] * share
    stored = (stored + jnp.arange(share)).reshape(1, enc)
    key_ids = jnp.sum(
        jnp.where(pack_index[0][:, None] == stored, enc_segments[0][:, None], 0),
        axis=0,
        keepdims=True,
    )
    size = share // PIECES
    mine = [enc_rows[0, i * size : (i + 1) * size] for i in range(PIECES)]

    def ring(values, *pairs):
        out = []
        for v in values:
            out.append(along(v, *pairs))
        return out

    up1 = ring(mine, (0, 1), (1, 2), (2, 3))
    down1 = ring(mine, (3, 2), (2, 1), (1, 0))
    up2 = ring(up1, (1, 2), (2, 3))
    down2 = ring(down1, (2, 1), (1, 0))
    third = [jnp.where(low, d, u) for u, d in zip(up2, down2)]
    third = ring(third, (2, 3), (1, 0))
    outer = (section == 0) | (section == 3)
    near_in = [jnp.where(low, d, u) for u, d in zip(up1, down1)]
    far_in = lax.optimization_barrier([jnp.where(low, u, d) for u, d in zip(up1, down1)])
    mid_in = [jnp.where(low, d, u) for u, d in zip(up2, down2)]
    last_in = [jnp.where(outer, t, f) for t, f in zip(third, far_in)]
    slots_in = [mine, near_in, mid_in, last_in]
    keys_values = []
    rows = share * n
    for slot, held in enumerate(slots_in):
        xs = [all_parts(v) for v in held]
        xs = [x[k] for k in range(n) for x in xs]
        if n > 2:
            xs = [jnp.concatenate(xs, axis=0)]
        project = pl.pallas_call(
            functools.partial(project_kernel, len(xs)),
            grid=(width // block,),
            in_specs=[pl.BlockSpec(x.shape, lambda i: (0, 0)) for x in xs]
            + [resident] * 2
            + [any_spec] * len(keys_values),
            out_specs=[pl.BlockSpec((rows, block), lambda i, slot=slot: (slot, i))] * 2,
            out_shape=[jax.ShapeDtypeStruct((enc, width), bf16)] * 2,
            scratch_shapes=[pltpu.VMEM((rows, model), bf16)],
            input_output_aliases={len(xs) + 2 + i: i for i in range(len(keys_values))},
            compiler_params=params,
            name="project",
        )
        keys_values = project(*xs, wk, wv, *keys_values)
    keys, values = keys_values

    probs = pl.pallas_call(
        probs_kernel,
        grid=(pairs, MICRO),
        in_specs=[
            pl.BlockSpec((m, PAIR), lambda p, i: (i, p)),
            pl.BlockSpec((enc, PAIR), lambda p, i: (0, p)),
            pl.BlockSpec((1, 2 * m, 1), lambda p, i: (i, 0, 0)),
            pl.BlockSpec((1, enc), lambda p, i: (0, 0)),
        ],
        out_specs=pl.BlockSpec((1, 1, 2 * m, enc), lambda p, i: (i, p, 0, 0)),
        out_shape=pltpu.MemorySpace.HBM((MICRO, pairs, 2 * m, enc), bf16),
        compiler_params=params,
        name="probs",
    )(queries, keys, token_ids, key_ids)

    weights = loaded(wo, wq, keys, values)

    def turn(t, ups, held, after):
        if parts == 1:
            ups = [jnp.concatenate(ups, axis=0)] if n > 1 else ups
        up_specs = [pl.BlockSpec(u.shape, lambda i, s: (0, 0)) for u in ups]
        return pl.pallas_call(
            functools.partial(turn_kernel, parts, r),
            grid_spec=pltpu.PrefetchScalarGridSpec(
                num_scalar_prefetch=1,
                grid=(width // block,),
                in_specs=up_specs
                + [resident] * 4
                + [
                    pl.BlockSpec((1, bp, 2 * m, enc), lambda i, s: (s[t, 0], i, 0, 0)),
                ]
                + [any_spec] * (len(held) + len(after)),
                out_specs=[
                    pl.BlockSpec((r, model), lambda i, s: (0, 0)),
                    pl.BlockSpec((m - r, model), lambda i, s: (0, 0)),
                    pl.BlockSpec((1, bp, 2 * m, enc), lambda i, s: (s[t, 1], i, 0, 0)),
                    pl.BlockSpec((1, m, block), lambda i, s: (s[t, 1], 0, i)),
                ],
                scratch_shapes=[pltpu.VMEM((m, model), f32)],
            ),
            out_shape=[
                jax.ShapeDtypeStruct((r, model), bf16),
                jax.ShapeDtypeStruct((m - r, model), bf16),
                pltpu.MemorySpace.HBM((MICRO + 1, pairs, 2 * m, enc), bf16),
                pltpu.MemorySpace.HBM((MICRO + 1, m, width), bf16),
            ],
            input_output_aliases={parts + 6 + i: 2 + i for i in range(len(held))},
            compiler_params=small,
            name="turn",
        )(slots, *ups, *weights, in_hbm(probs), *map(in_hbm, held), *map(in_hbm, after))

    def norm_back(t, got, own_part, up_own, held):
        row_spec = pl.BlockSpec((r, model), lambda i, s: (0, 0))
        k = len(got)
        return pl.pallas_call(
            functools.partial(norm_kernel, k),
            grid_spec=pltpu.PrefetchScalarGridSpec(
                num_scalar_prefetch=1,
                grid=(1,),
                in_specs=[row_spec] * (k + 2)
                + [
                    pl.BlockSpec((r, model), lambda i, s: (s[t, 0], 0)),
                    pl.BlockSpec((1, model), lambda i, s: (0, 0)),
                ]
                + [any_spec] * len(held),
                out_specs=[row_spec, pl.BlockSpec((r, model), lambda i, s: (s[t, 1], 0))],
            ),
            out_shape=[
                jax.ShapeDtypeStruct((r, model), bf16),
                pltpu.MemorySpace.HBM(((MICRO + 1) * r, model), bf16),
            ],
            input_output_aliases={k + 5: 1} if held else {},
            compiler_params=small,
            name="norm",
        )(slots, *got, own_part, up_own, in_hbm(x_own), gain, *map(in_hbm, held))

    held, dec_held = [], []
    is_last = section == sections - 1
    hops = {}
    turns = MICRO + SKEW * (sections - 1)
    micro = jnp.arange(turns, dtype=jnp.int32) - SKEW * (sections - 1 - section)
    read = jnp.clip(micro, 0, MICRO - 1)
    slots = jnp.stack([read, jnp.where(micro == read, read, MICRO)], axis=1)
    for t in range(turns):
        if t < MICRO:
            up_own = cotangent[0, t * r : (t + 1) * r]
            if t >= SKEW:
                up_own, _ = lax.optimization_barrier((up_own, own_part))
                up_own = jnp.where(is_last, up_own, hops[t - SKEW])
        else:
            up_own = hops[t - SKEW]
        ups = all_parts(up_own)
        own_part, other, *held = turn(t, ups, held, dec_held)
        got = [
            shifted(other if n == 2 else other[(k - 1) * r : k * r], -k) for k in range(1, n)
        ]
        mine, *dec_held = norm_back(t, got, own_part, up_own, dec_held)
        if t + SKEW < turns:
            hops[t] = along(mine, (3, 2), (2, 1), (1, 0))

    kg, vg = pl.pallas_call(
        functools.partial(grads_kernel, MICRO),
        grid=(pairs,),
        in_specs=[
            pl.BlockSpec((MICRO, 1, 2 * m, enc), lambda p: (0, p, 0, 0)),
            pl.BlockSpec((MICRO, 1, 2 * m, enc), lambda p: (0, p, 0, 0)),
            pl.BlockSpec((tokens, PAIR), lambda p: (0, p)),
            pl.BlockSpec((MICRO, m, PAIR), lambda p: (0, 0, p)),
        ],
        out_specs=[pl.BlockSpec((enc, PAIR), lambda p: (0, p))] * 2,
        out_shape=[jax.ShapeDtypeStruct((enc, width), bf16)] * 2,
        compiler_params=params,
        name="grads",
    )(*map(in_hbm, (held[0], probs, queries, held[1])))

    out_block = min(OUT_BLOCK, model)

    def back(slot):
        own_part, other = back_call(slot)
        return summed_parts(own_part, other)

    def back_call(slot):
        return pl.pallas_call(
            back_kernel,
            grid=(model // out_block,),
            in_specs=[pl.BlockSpec((rows, width), lambda i: (slot, 0))] * 2
            + [resident] * 2,
            out_specs=[
                pl.BlockSpec((share, out_block), lambda i: (0, i)),
                pl.BlockSpec((rows - share, out_block), lambda i: (0, i)),
            ],
            out_shape=[
                jax.ShapeDtypeStruct((share, model), bf16),
                jax.ShapeDtypeStruct((rows - share, model), bf16),
            ],
            compiler_params=params,
            name="back",
        )(kg, vg, wk, wv)

    def summed_parts(own_part, other):
        totals = []
        for i in range(PIECES):
            total = own_part[i * size : (i + 1) * size].astype(f32)
            for k in range(1, n):
                first = (k - 1) * share + i * size
                got = shifted(other[first : first + size], -k)
                total = total + got.astype(f32)
            totals.append(total)
        return totals

    far, mid = back(3), back(2)
    got = []
    for v in far:
        got.append(along(v.astype(bf16), (0, 1), (3, 2)))
    near = back(1)
    up2, down2 = [], []
    for v, g in zip(mid, got):
        v = (v + g.astype(f32)).astype(bf16)
        up2.append(along(v, (0, 1), (1, 2)))
        down2.append(along(v, (3, 2), (2, 1)))
    here = back(0)
    enc_share = []
    for i in range(PIECES):
        up3 = jnp.where(section == 2, far[i], near[i]) + up2[i].astype(f32)
        down3 = jnp.where(section == 1, far[i], near[i]) + down2[i].astype(f32)
        up3 = along(up3.astype(bf16), (0, 1), (1, 2), (2, 3))
        down3 = along(down3.astype(bf16), (3, 2), (2, 1), (1, 0))
        enc_share.append(here[i] + up3.astype(f32) + down3.astype(f32))
    enc_share = jnp.concatenate(enc_share, axis=0)
    return dec_held[0][:own][None, None], enc_share[None]


def solution(mesh):
    in_specs = (
        P("dp", ("section", "mp"), None),
        P("dp", None),
        P("dp", None),
        P("dp", None),
        P("dp", "section", "mp", None),
        P("section", None),
        P("section", None, "mp"),
        P("section", None, "mp"),
        P("section", None, "mp"),
        P("section", "mp", None),
        P("dp", "mp", None),
    )
    out_specs = (P("dp", "section", "mp", None), P("dp", ("section", "mp"), None))
    return jax.shard_map(
        all_of_it, mesh=mesh, in_specs=in_specs, out_specs=out_specs, check_vma=False
    )
```

```python
import functools

import jax
import jax.numpy as jnp
from jax import lax
from jax.experimental import pallas as pl
from jax.experimental.pallas import tpu as pltpu
from jax.sharding import PartitionSpec as P

HD = 64
PAIR = 2 * HD
MICRO = 4
SKEW = 2
PIECES = 1
BLOCK = 512
OUT_BLOCK = 512
SLOTS = ((0, 1, 2, 3), (1, 2, 1, 2), (2, 3, 0, 1), (3, 0, 3, 0))

epsilon = 1e-06
masked_value = -1e30
f32 = jnp.float32
bf16 = jnp.bfloat16
NT = (((1,), (1,)), ((), ()))
NN = (((1,), (0,)), ((), ()))


def dot(a, b, dims):
    return lax.dot_general(a, b, dims, preferred_element_type=f32)


def stacked(x):
    lane = lax.broadcasted_iota(jnp.int32, x.shape, 1)
    zero = jnp.zeros_like(x)
    return jnp.concatenate(
        [jnp.where(lane < HD, x, zero), jnp.where(lane >= HD, x, zero)], axis=0
    )


def probs_kernel(q_ref, k_ref, tok_ref, key_ref, wo_ref, wq_ref, p_ref, wo_out, wq_out, sems):
    first = (pl.program_id(0) == 0) & (pl.program_id(1) == 0)
    last = pl.program_id(0) == pl.num_programs(0) - 1
    last = last & (pl.program_id(1) == pl.num_programs(1) - 1)
    copies = [
        pltpu.make_async_copy(wo_ref, wo_out, sems.at[0]),
        pltpu.make_async_copy(wq_ref, wq_out, sems.at[1]),
    ]

    @pl.when(first)
    def _():
        for copy in copies:
            copy.start()

    q = stacked(q_ref[...].astype(f32) * (HD**-0.5)).astype(bf16)
    s = dot(q, k_ref[...], NT)
    s = jnp.where(tok_ref[0] == key_ref[...], s, masked_value)
    e = jnp.exp(s - jnp.max(s, axis=-1, keepdims=True))
    total = jnp.sum(e, axis=-1, keepdims=True)
    p_ref[pl.program_id(1), pl.program_id(0)] = (e * (1.0 / total)).astype(bf16)

    @pl.when(last)
    def _():
        for copy in copies:
            copy.wait()


def project_kernel(count, slot, block, *refs):
    x_refs = refs[:count]
    wk_ref, wv_ref = refs[count : count + 2]
    k_ref, v_ref, x_all = refs[-3:]

    @pl.when(pl.program_id(0) == 0)
    def _():
        start = 0
        for x in x_refs:
            x_all[start : start + x.shape[0]] = x[...]
            start += x.shape[0]

    cols = pl.ds(pl.multiple_of(pl.program_id(0) * block, block), block)
    rows = slice(slot * x_all.shape[0], (slot + 1) * x_all.shape[0])
    k_ref[rows, cols] = dot(x_all[...], wk_ref[:, cols], NN).astype(bf16)
    v_ref[rows, cols] = dot(x_all[...], wv_ref[:, cols], NN).astype(bf16)


def back_kernel(kg_ref, vg_ref, wk_ref, wv_ref, own_ref, other_ref):
    out = dot(kg_ref[...], wk_ref[...], NT) + dot(vg_ref[...], wv_ref[...], NT)
    rows = own_ref.shape[0]
    own_ref[...] = out[:rows].astype(bf16)
    other_ref[...] = out[rows:].astype(bf16)


def turn_kernel(parts, own_rows, t, block, slots, *refs):
    read, write = slots[t, 0], slots[t, 1]
    up_refs = refs[:parts]
    wo_ref, wq_ref, k_ref, v_ref, p_ref = refs[parts : parts + 5]
    own_ref, other_ref, ds_ref, ag_ref, acc_ref = refs[-5:]
    step = pl.program_id(0)
    start = pl.multiple_of(step * block, block)
    up = up_refs[0][...] if parts == 1 else jnp.concatenate([r[...] for r in up_refs], axis=0)
    rows = up.shape[0]
    grads = dot(up, wo_ref[pl.ds(start, block), :], NT).astype(bf16)
    ag_ref[write, :, pl.ds(start, block)] = grads
    wide = grads.astype(f32)
    lane = lax.broadcasted_iota(jnp.int32, (rows, PAIR), 1)
    pieces = []
    for pair in range(grads.shape[1] // PAIR):
        cols = pl.ds(pl.multiple_of(start + pair * PAIR, PAIR), PAIR)
        here = wide[:, pair * PAIR : (pair + 1) * PAIR]
        pg = dot(stacked(here).astype(bf16), v_ref[:, cols], NT)
        place = step * (block // PAIR) + pair
        p = p_ref[read, place].astype(f32)
        mean = jnp.sum(pg * p, axis=-1, keepdims=True)
        ds = (p * (pg - mean)).astype(bf16)
        ds_ref[write, place] = ds
        both = dot(ds, k_ref[:, cols], NN)
        mine = jnp.where(lane < HD, both[:rows], both[rows:]) * (HD**-0.5)
        pieces.append(mine.astype(bf16))
    qg = pieces[0] if len(pieces) == 1 else jnp.concatenate(pieces, axis=1)
    partial = dot(qg, wq_ref[:, pl.ds(start, block)], NT)

    @pl.when(step == 0)
    def _():
        acc_ref[...] = partial

    @pl.when(step > 0)
    def _():
        acc_ref[...] += partial

    @pl.when(step == pl.num_programs(0) - 1)
    def _():
        own_ref[...] = acc_ref[:own_rows].astype(bf16)
        other_ref[...] = acc_ref[own_rows:].astype(bf16)


def norm_kernel(received, t, slots, *refs):
    got_refs = refs[:received]
    own_ref, up_ref, x_ref, gain_ref = refs[received : received + 4]
    mine_ref, all_ref = refs[-2:]
    rows = mine_ref.shape[0]
    x = x_ref[pl.ds(pl.multiple_of(slots[t, 0] * rows, rows), rows), :].astype(f32)
    recip = lax.rsqrt(jnp.mean(x * x, axis=-1, keepdims=True) + epsilon)
    unit = x * recip
    summed = own_ref[...].astype(f32)
    for got in got_refs:
        summed = summed + got[...].astype(f32)
    scaled = summed * gain_ref[...]
    out = up_ref[...].astype(f32) + recip * (
        scaled - unit * jnp.mean(scaled * unit, axis=-1, keepdims=True)
    )
    out = out.astype(bf16)
    mine_ref[...] = out
    all_ref[pl.ds(pl.multiple_of(slots[t, 1] * rows, rows), rows), :] = out


def grads_kernel(micro, ds_ref, p_ref, q_ref, ag_ref, kg_ref, vg_ref):
    rows = ag_ref.shape[1]
    pair = pl.program_id(0)
    cols = pl.ds(pl.multiple_of(pair * PAIR, PAIR), PAIR)
    q = jnp.concatenate(
        [stacked(q_ref[i * rows : (i + 1) * rows, :].astype(f32)) for i in range(micro)], axis=0
    )
    ag = jnp.concatenate(
        [stacked(ag_ref[i, :, cols].astype(f32)) for i in range(micro)], axis=0
    )
    ds = jnp.concatenate([ds_ref[i, pair] for i in range(micro)], axis=0)
    p = jnp.concatenate([p_ref[i, pair] for i in range(micro)], axis=0)
    kg = dot(q.T.astype(bf16), ds, NN) * (HD**-0.5)
    vg = dot(ag.T.astype(bf16), p, NN)
    kg_ref[...] = kg.T.astype(bf16)
    vg_ref[...] = vg.T.astype(bf16)


def all_of_it(
    enc_rows,
    pack_index,
    enc_segments,
    dec_segments,
    dec_inputs,
    norm_gain,
    w_query,
    w_key,
    w_value,
    w_out,
    cotangent,
):
    wq, wk, wv, wo = w_query[0], w_key[0], w_value[0], w_out[0]
    gain = norm_gain.astype(f32)
    model, width = wq.shape
    pairs = width // PAIR
    n = lax.axis_size("mp")
    sections = lax.axis_size("section")
    me = lax.axis_index("mp")
    section = lax.axis_index("section")
    assert sections == len(SLOTS)
    share = enc_rows.shape[1]
    enc = share * n * sections
    own = dec_inputs.shape[2]
    r = own // MICRO
    m = r * n
    tokens = own * n
    params = pltpu.CompilerParams(vmem_limit_bytes=24 * 1024 * 1024)
    small = pltpu.CompilerParams(vmem_limit_bytes=12 * 1024 * 1024)
    least = pltpu.CompilerParams(vmem_limit_bytes=8 * 1024 * 1024)

    def shifted(x, by):
        return lax.ppermute(x, "mp", [((i + by) % n, i) for i in range(n)])

    def along(x, *pairs):
        return lax.ppermute(x, "section", pairs)

    low = section < 2
    block = min(BLOCK, width)
    parts = 2 if n == 2 else 1
    any_spec = pl.BlockSpec(memory_space=pl.ANY)
    resident = pl.BlockSpec(memory_space=pltpu.MemorySpace.VMEM)

    def in_hbm(x):
        return pltpu.with_memory_space_constraint(x, pltpu.MemorySpace.HBM)

    def in_vmem(shape):
        return pltpu.MemorySpace.VMEM(shape, bf16)

    def all_parts(x):
        return [x] + [shifted(x, k) for k in range(1, n)]

    x_own = dec_inputs[0, 0]
    x_all = jnp.stack([v.reshape(MICRO, r, model) for v in all_parts(x_own)], axis=1)
    x_all = x_all.reshape(tokens, model).astype(f32)
    recip = lax.rsqrt(jnp.mean(x_all * x_all, axis=-1, keepdims=True) + epsilon)
    normed = (x_all * recip * gain).astype(bf16)
    queries = dot(normed, wq, NN).astype(bf16)
    token_ids = dec_segments[0].reshape(n, MICRO, r)
    order = jnp.remainder(me + jnp.arange(n), n)
    token_ids = jnp.take(token_ids, order, axis=0).transpose(1, 0, 2).reshape(MICRO, m)
    token_ids = jnp.concatenate([token_ids, token_ids], axis=1)[:, :, None]

    blocks = jnp.asarray(SLOTS, jnp.int32)[:, section]
    stored = (blocks[:, None] * n + order[None, :])[:, :, None] * share
    stored = (stored + jnp.arange(share)).reshape(1, enc)
    key_ids = jnp.sum(
        jnp.where(pack_index[0][:, None] == stored, enc_segments[0][:, None], 0),
        axis=0,
        keepdims=True,
    )
    turns = MICRO + SKEW * (sections - 1)
    micro = jnp.arange(turns, dtype=jnp.int32) - SKEW * (sections - 1 - section)
    read = jnp.clip(micro, 0, MICRO - 1)
    slots = jnp.stack([read, jnp.where(micro == read, read, MICRO)], axis=1)
    outer = (section == 0) | (section == 3)
    is_last = section == sections - 1
    wk, wv, low, outer, is_last, slots = lax.optimization_barrier(
        (wk, wv, low, outer, is_last, slots)
    )
    size = share // PIECES
    mine = [enc_rows[0, i * size : (i + 1) * size] for i in range(PIECES)]

    def ring(values, *pairs):
        out = []
        for v in values:
            out.append(along(v, *pairs))
        return out

    up1 = ring(mine, (0, 1), (1, 2), (2, 3))
    down1 = ring(mine, (3, 2), (2, 1), (1, 0))
    up2 = ring(up1, (1, 2), (2, 3))
    down2 = ring(down1, (2, 1), (1, 0))
    third = [jnp.where(low, d, u) for u, d in zip(up2, down2)]
    third = ring(third, (2, 3), (1, 0))
    near_in = [jnp.where(low, d, u) for u, d in zip(up1, down1)]
    far_in = lax.optimization_barrier([jnp.where(low, u, d) for u, d in zip(up1, down1)])
    mid_in = [jnp.where(low, d, u) for u, d in zip(up2, down2)]
    last_in = [jnp.where(outer, t, f) for t, f in zip(third, far_in)]
    slots_in = [mine, near_in, mid_in, last_in]
    keys_values = []
    rows = share * n
    for slot, held in enumerate(slots_in):
        xs = [all_parts(v) for v in held]
        xs = [x[k] for k in range(n) for x in xs]
        early = [] if slot else [slots, key_ids, token_ids]
        if n > 2:
            xs = [jnp.concatenate(xs, axis=0)]
        project = pl.pallas_call(
            functools.partial(project_kernel, len(xs), slot, block),
            grid=(width // block,),
            in_specs=[pl.BlockSpec(x.shape, lambda i: (0, 0)) for x in xs]
            + [resident] * (2 + len(keys_values))
            + [any_spec] * len(early),
            out_specs=[resident] * 2,
            out_shape=[in_vmem((enc, width))] * 2,
            scratch_shapes=[pltpu.VMEM((rows, model), bf16)],
            input_output_aliases={len(xs) + 2 + i: i for i in range(len(keys_values))},
            compiler_params=small,
            name="project",
        )
        keys_values = project(*xs, wk, wv, *keys_values, *early)
    keys, values = keys_values

    probs, *weights = pl.pallas_call(
        probs_kernel,
        grid=(pairs, MICRO),
        in_specs=[
            pl.BlockSpec((m, PAIR), lambda p, i: (i, p)),
            pl.BlockSpec((enc, PAIR), lambda p, i: (0, p)),
            pl.BlockSpec((1, 2 * m, 1), lambda p, i: (i, 0, 0)),
            pl.BlockSpec((1, enc), lambda p, i: (0, 0)),
            any_spec,
            any_spec,
        ],
        out_specs=[resident] * 3,
        out_shape=[
            in_vmem((MICRO, pairs, 2 * m, enc)),
            in_vmem(wo.shape),
            in_vmem(wq.shape),
        ],
        scratch_shapes=[pltpu.SemaphoreType.DMA((2,))],
        compiler_params=small,
        name="probs",
    )(queries, keys, token_ids, key_ids, in_hbm(wo), in_hbm(wq))


    def turn(t, ups, held, after):
        if parts == 1:
            ups = [jnp.concatenate(ups, axis=0)] if n > 1 else ups
        return pl.pallas_call(
            functools.partial(turn_kernel, parts, r, t, block),
            grid_spec=pltpu.PrefetchScalarGridSpec(
                num_scalar_prefetch=1,
                grid=(width // block,),
                in_specs=[resident] * (parts + 5 + len(held)) + [any_spec] * len(after),
                out_specs=[resident] * 4,
                scratch_shapes=[pltpu.VMEM((m, model), f32)],
            ),
            out_shape=[
                in_vmem((r, model)),
                in_vmem((m - r, model)),
                in_vmem((MICRO + 1, pairs, 2 * m, enc)),
                in_vmem((MICRO + 1, m, width)),
            ],
            input_output_aliases={parts + 6 + i: 2 + i for i in range(len(held))},
            compiler_params=least,
            name="turn",
        )(slots, *ups, *weights, keys, values, probs, *held, *after)

    def norm_back(t, got, own_part, up_own, held):
        k = len(got)
        return pl.pallas_call(
            functools.partial(norm_kernel, k, t),
            grid_spec=pltpu.PrefetchScalarGridSpec(
                num_scalar_prefetch=1,
                grid=(1,),
                in_specs=[resident] * (k + 4 + len(held)),
                out_specs=[resident] * 2,
            ),
            out_shape=[in_vmem((r, model)), in_vmem(((MICRO + 1) * r, model))],
            input_output_aliases={k + 5: 1} if held else {},
            compiler_params=least,
            name="norm",
        )(slots, *got, own_part, up_own, x_own, gain, *held)

    held, dec_held = [], []
    hops = {}
    for t in range(turns):
        if t < MICRO:
            up_own = cotangent[0, t * r : (t + 1) * r]
            if t >= SKEW:
                up_own, _ = lax.optimization_barrier((up_own, own_part))
                up_own = jnp.where(is_last, up_own, hops[t - SKEW])
        else:
            up_own = hops[t - SKEW]
        ups = all_parts(up_own)
        own_part, other, *held = turn(t, ups, held, dec_held)
        got = [
            shifted(other if n == 2 else other[(k - 1) * r : k * r], -k) for k in range(1, n)
        ]
        mine, *dec_held = norm_back(t, got, own_part, up_own, dec_held)
        if t + SKEW < turns:
            hops[t] = along(mine, (3, 2), (2, 1), (1, 0))

    kg, vg = pl.pallas_call(
        functools.partial(grads_kernel, MICRO),
        grid=(pairs,),
        in_specs=[
            resident,
            resident,
            pl.BlockSpec((tokens, PAIR), lambda p: (0, p)),
            resident,
        ],
        out_specs=[pl.BlockSpec((enc, PAIR), lambda p: (0, p))] * 2,
        out_shape=[jax.ShapeDtypeStruct((enc, width), bf16)] * 2,
        compiler_params=small,
        name="grads",
    )(held[0], probs, in_hbm(queries), held[1])

    out_block = min(OUT_BLOCK, model)

    def back(slot):
        own_part, other = back_call(slot)
        return summed_parts(own_part, other)

    def back_call(slot):
        return pl.pallas_call(
            back_kernel,
            grid=(model // out_block,),
            in_specs=[pl.BlockSpec((rows, width), lambda i: (slot, 0))] * 2
            + [pl.BlockSpec((out_block, width), lambda i: (i, 0))] * 2,
            out_specs=[
                pl.BlockSpec((share, out_block), lambda i: (0, i)),
                pl.BlockSpec((rows - share, out_block), lambda i: (0, i)),
            ],
            out_shape=[
                jax.ShapeDtypeStruct((share, model), bf16),
                jax.ShapeDtypeStruct((rows - share, model), bf16),
            ],
            compiler_params=small,
            name="back",
        )(kg, vg, in_hbm(w_key[0]), in_hbm(w_value[0]))

    def summed_parts(own_part, other):
        totals = []
        for i in range(PIECES):
            total = own_part[i * size : (i + 1) * size].astype(f32)
            for k in range(1, n):
                first = (k - 1) * share + i * size
                got = shifted(other[first : first + size], -k)
                total = total + got.astype(f32)
            totals.append(total)
        return totals

    far, mid = back(3), back(2)
    got = []
    for v in far:
        got.append(along(v.astype(bf16), (0, 1), (3, 2)))
    near = back(1)
    up2, down2 = [], []
    for v, g in zip(mid, got):
        v = (v + g.astype(f32)).astype(bf16)
        up2.append(along(v, (0, 1), (1, 2)))
        down2.append(along(v, (3, 2), (2, 1)))
    here = back(0)
    enc_share = []
    for i in range(PIECES):
        up3 = jnp.where(section == 2, far[i], near[i]) + up2[i].astype(f32)
        down3 = jnp.where(section == 1, far[i], near[i]) + down2[i].astype(f32)
        up3 = along(up3.astype(bf16), (0, 1), (1, 2), (2, 3))
        down3 = along(down3.astype(bf16), (3, 2), (2, 1), (1, 0))
        enc_share.append(here[i] + up3.astype(f32) + down3.astype(f32))
    enc_share = jnp.concatenate(enc_share, axis=0)
    return dec_held[0][:own][None, None], enc_share[None]


def solution(mesh):
    in_specs = (
        P("dp", ("section", "mp"), None),
        P("dp", None),
        P("dp", None),
        P("dp", None),
        P("dp", "section", "mp", None),
        P("section", None),
        P("section", None, "mp"),
        P("section", None, "mp"),
        P("section", None, "mp"),
        P("section", "mp", None),
        P("dp", "mp", None),
    )
    out_specs = (P("dp", "section", "mp", None), P("dp", ("section", "mp"), None))
    return jax.shard_map(
        all_of_it, mesh=mesh, in_specs=in_specs, out_specs=out_specs, check_vma=False
    )
```

```python
import functools

import jax
import jax.numpy as jnp
from jax import lax
from jax.experimental import pallas as pl
from jax.experimental.pallas import tpu as pltpu
from jax.sharding import PartitionSpec as P

HD = 64
PAIR = 2 * HD
MICRO = 4
SKEW = 2
PIECES = 2
BLOCK = 512
OUT_BLOCK = 512
SLOTS = ((0, 1, 2, 3), (1, 2, 1, 2), (2, 3, 0, 1), (3, 0, 3, 0))

epsilon = 1e-06
masked_value = -1e30
f32 = jnp.float32
bf16 = jnp.bfloat16
NT = (((1,), (1,)), ((), ()))
NN = (((1,), (0,)), ((), ()))


def dot(a, b, dims):
    return lax.dot_general(a, b, dims, preferred_element_type=f32)


def stacked(x):
    lane = lax.broadcasted_iota(jnp.int32, x.shape, 1)
    zero = jnp.zeros_like(x)
    return jnp.concatenate(
        [jnp.where(lane < HD, x, zero), jnp.where(lane >= HD, x, zero)], axis=0
    )


def probs_kernel(q_ref, k_ref, tok_ref, key_ref, wo_ref, wq_ref, p_ref, wo_out, wq_out, sems):
    first = (pl.program_id(0) == 0) & (pl.program_id(1) == 0)
    last = pl.program_id(0) == pl.num_programs(0) - 1
    last = last & (pl.program_id(1) == pl.num_programs(1) - 1)
    copies = [
        pltpu.make_async_copy(wo_ref, wo_out, sems.at[0]),
        pltpu.make_async_copy(wq_ref, wq_out, sems.at[1]),
    ]

    @pl.when(first)
    def _():
        for copy in copies:
            copy.start()

    q = stacked(q_ref[...].astype(f32) * (HD**-0.5)).astype(bf16)
    s = dot(q, k_ref[...], NT)
    s = jnp.where(tok_ref[0] == key_ref[...], s, masked_value)
    e = jnp.exp(s - jnp.max(s, axis=-1, keepdims=True))
    total = jnp.sum(e, axis=-1, keepdims=True)
    p_ref[pl.program_id(1), pl.program_id(0)] = (e * (1.0 / total)).astype(bf16)

    @pl.when(last)
    def _():
        for copy in copies:
            copy.wait()


def project_kernel(count, slot, block, *refs):
    x_refs = refs[:count]
    wk_ref, wv_ref = refs[count : count + 2]
    k_ref, v_ref, x_all = refs[-3:]

    @pl.when(pl.program_id(0) == 0)
    def _():
        start = 0
        for x in x_refs:
            x_all[start : start + x.shape[0]] = x[...]
            start += x.shape[0]

    cols = pl.ds(pl.multiple_of(pl.program_id(0) * block, block), block)
    rows = slice(slot * x_all.shape[0], (slot + 1) * x_all.shape[0])
    k_ref[rows, cols] = dot(x_all[...], wk_ref[:, cols], NN).astype(bf16)
    v_ref[rows, cols] = dot(x_all[...], wv_ref[:, cols], NN).astype(bf16)


def back_kernel(kg_ref, vg_ref, wk_ref, wv_ref, *out_refs):
    out = dot(kg_ref[...], wk_ref[...], NT) + dot(vg_ref[...], wv_ref[...], NT)
    rows = out_refs[0].shape[0]
    for i, ref in enumerate(out_refs):
        ref[...] = out[i * rows : (i + 1) * rows].astype(bf16)


def turn_kernel(parts, own_rows, t, block, slots, *refs):
    read, write = slots[t, 0], slots[t, 1]
    up_refs = refs[:parts]
    wo_ref, wq_ref, k_ref, v_ref, p_ref = refs[parts : parts + 5]
    own_ref, other_ref, ds_ref, ag_ref, acc_ref = refs[-5:]
    step = pl.program_id(0)
    start = pl.multiple_of(step * block, block)
    up = up_refs[0][...] if parts == 1 else jnp.concatenate([r[...] for r in up_refs], axis=0)
    rows = up.shape[0]
    grads = dot(up, wo_ref[pl.ds(start, block), :], NT).astype(bf16)
    ag_ref[write, :, pl.ds(start, block)] = grads
    wide = grads.astype(f32)
    lane = lax.broadcasted_iota(jnp.int32, (rows, PAIR), 1)
    pieces = []
    for pair in range(grads.shape[1] // PAIR):
        cols = pl.ds(pl.multiple_of(start + pair * PAIR, PAIR), PAIR)
        here = wide[:, pair * PAIR : (pair + 1) * PAIR]
        pg = dot(stacked(here).astype(bf16), v_ref[:, cols], NT)
        place = step * (block // PAIR) + pair
        p = p_ref[read, place].astype(f32)
        mean = jnp.sum(pg * p, axis=-1, keepdims=True)
        ds = (p * (pg - mean)).astype(bf16)
        ds_ref[write, place] = ds
        both = dot(ds, k_ref[:, cols], NN)
        mine = jnp.where(lane < HD, both[:rows], both[rows:]) * (HD**-0.5)
        pieces.append(mine.astype(bf16))
    qg = pieces[0] if len(pieces) == 1 else jnp.concatenate(pieces, axis=1)
    partial = dot(qg, wq_ref[:, pl.ds(start, block)], NT)

    @pl.when(step == 0)
    def _():
        acc_ref[...] = partial

    @pl.when(step > 0)
    def _():
        acc_ref[...] += partial

    @pl.when(step == pl.num_programs(0) - 1)
    def _():
        own_ref[...] = acc_ref[:own_rows].astype(bf16)
        other_ref[...] = acc_ref[own_rows:].astype(bf16)


def norm_kernel(received, t, slots, *refs):
    got_refs = refs[:received]
    own_ref, up_ref, x_ref, gain_ref = refs[received : received + 4]
    mine_ref, all_ref = refs[-2:]
    rows = mine_ref.shape[0]
    x = x_ref[pl.ds(pl.multiple_of(slots[t, 0] * rows, rows), rows), :].astype(f32)
    recip = lax.rsqrt(jnp.mean(x * x, axis=-1, keepdims=True) + epsilon)
    unit = x * recip
    summed = own_ref[...].astype(f32)
    for got in got_refs:
        summed = summed + got[...].astype(f32)
    scaled = summed * gain_ref[...]
    out = up_ref[...].astype(f32) + recip * (
        scaled - unit * jnp.mean(scaled * unit, axis=-1, keepdims=True)
    )
    out = out.astype(bf16)
    mine_ref[...] = out
    all_ref[pl.ds(pl.multiple_of(slots[t, 1] * rows, rows), rows), :] = out


def grads_kernel(micro, ds_ref, p_ref, q_ref, ag_ref, kg_ref, vg_ref):
    rows = ag_ref.shape[1]
    pair = pl.program_id(0)
    cols = pl.ds(pl.multiple_of(pair * PAIR, PAIR), PAIR)
    q = jnp.concatenate(
        [stacked(q_ref[i * rows : (i + 1) * rows, :].astype(f32)) for i in range(micro)], axis=0
    )
    ag = jnp.concatenate(
        [stacked(ag_ref[i, :, cols].astype(f32)) for i in range(micro)], axis=0
    )
    ds = jnp.concatenate([ds_ref[i, pair] for i in range(micro)], axis=0)
    p = jnp.concatenate([p_ref[i, pair] for i in range(micro)], axis=0)
    kg = dot(q.T.astype(bf16), ds, NN) * (HD**-0.5)
    vg = dot(ag.T.astype(bf16), p, NN)
    kg_ref[...] = kg.T.astype(bf16)
    vg_ref[...] = vg.T.astype(bf16)


def all_of_it(
    enc_rows,
    pack_index,
    enc_segments,
    dec_segments,
    dec_inputs,
    norm_gain,
    w_query,
    w_key,
    w_value,
    w_out,
    cotangent,
):
    wq, wk, wv, wo = w_query[0], w_key[0], w_value[0], w_out[0]
    gain = norm_gain.astype(f32)
    model, width = wq.shape
    pairs = width // PAIR
    n = lax.axis_size("mp")
    sections = lax.axis_size("section")
    me = lax.axis_index("mp")
    section = lax.axis_index("section")
    assert sections == len(SLOTS)
    share = enc_rows.shape[1]
    enc = share * n * sections
    own = dec_inputs.shape[2]
    r = own // MICRO
    m = r * n
    tokens = own * n
    params = pltpu.CompilerParams(vmem_limit_bytes=24 * 1024 * 1024)
    small = pltpu.CompilerParams(vmem_limit_bytes=10 * 1024 * 1024)
    least = pltpu.CompilerParams(vmem_limit_bytes=5 * 1024 * 1024)

    def shifted(x, by):
        return lax.ppermute(x, "mp", [((i + by) % n, i) for i in range(n)])

    def along(x, *pairs):
        return lax.ppermute(x, "section", pairs)

    low = section < 2
    block = min(BLOCK, width)
    parts = 2 if n == 2 else 1
    any_spec = pl.BlockSpec(memory_space=pl.ANY)
    resident = pl.BlockSpec(memory_space=pltpu.MemorySpace.VMEM)

    def in_hbm(x):
        return pltpu.with_memory_space_constraint(x, pltpu.MemorySpace.HBM)

    def in_vmem(shape):
        return pltpu.MemorySpace.VMEM(shape, bf16)

    def all_parts(x):
        return [x] + [shifted(x, k) for k in range(1, n)]

    x_own = dec_inputs[0, 0]
    x_all = jnp.stack([v.reshape(MICRO, r, model) for v in all_parts(x_own)], axis=1)
    x_all = x_all.reshape(tokens, model).astype(f32)
    recip = lax.rsqrt(jnp.mean(x_all * x_all, axis=-1, keepdims=True) + epsilon)
    normed = (x_all * recip * gain).astype(bf16)
    queries = dot(normed, wq, NN).astype(bf16)
    token_ids = dec_segments[0].reshape(n, MICRO, r)
    order = jnp.remainder(me + jnp.arange(n), n)
    token_ids = jnp.take(token_ids, order, axis=0).transpose(1, 0, 2).reshape(MICRO, m)
    token_ids = jnp.concatenate([token_ids, token_ids], axis=1)[:, :, None]

    blocks = jnp.asarray(SLOTS, jnp.int32)[:, section]
    stored = (blocks[:, None] * n + order[None, :])[:, :, None] * share
    stored = (stored + jnp.arange(share)).reshape(1, enc)
    key_ids = jnp.sum(
        jnp.where(pack_index[0][:, None] == stored, enc_segments[0][:, None], 0),
        axis=0,
        keepdims=True,
    )
    turns = MICRO + SKEW * (sections - 1)
    micro = jnp.arange(turns, dtype=jnp.int32) - SKEW * (sections - 1 - section)
    read = jnp.clip(micro, 0, MICRO - 1)
    slots = jnp.stack([read, jnp.where(micro == read, read, MICRO)], axis=1)
    outer = (section == 0) | (section == 3)
    is_last = section == sections - 1
    wk, wv, low, outer, is_last, slots = lax.optimization_barrier(
        (wk, wv, low, outer, is_last, slots)
    )
    size = share // PIECES
    mine = [enc_rows[0, i * size : (i + 1) * size] for i in range(PIECES)]

    def ring(values, *pairs):
        out = []
        for v in values:
            out.append(along(v, *pairs))
        return out

    up1 = ring(mine, (0, 1), (1, 2), (2, 3))
    down1 = ring(mine, (3, 2), (2, 1), (1, 0))
    up2 = ring(up1, (1, 2), (2, 3))
    down2 = ring(down1, (2, 1), (1, 0))
    third = [jnp.where(low, d, u) for u, d in zip(up2, down2)]
    third = ring(third, (2, 3), (1, 0))
    near_in = [jnp.where(low, d, u) for u, d in zip(up1, down1)]
    far_in = lax.optimization_barrier([jnp.where(low, u, d) for u, d in zip(up1, down1)])
    mid_in = [jnp.where(low, d, u) for u, d in zip(up2, down2)]
    last_in = [jnp.where(outer, t, f) for t, f in zip(third, far_in)]
    slots_in = [mine, near_in, mid_in, last_in]
    keys_values = []
    rows = share * n
    for slot, held in enumerate(slots_in):
        xs = [all_parts(v) for v in held]
        xs = [x[k] for k in range(n) for x in xs]
        early = [] if slot else [slots, key_ids, token_ids]
        if n > 2:
            xs = [jnp.concatenate(xs, axis=0)]
        project = pl.pallas_call(
            functools.partial(project_kernel, len(xs), slot, block),
            grid=(width // block,),
            in_specs=[pl.BlockSpec(x.shape, lambda i: (0, 0)) for x in xs]
            + [resident] * (2 + len(keys_values))
            + [any_spec] * len(early),
            out_specs=[resident] * 2,
            out_shape=[in_vmem((enc, width))] * 2,
            scratch_shapes=[pltpu.VMEM((rows, model), bf16)],
            input_output_aliases={len(xs) + 2 + i: i for i in range(len(keys_values))},
            compiler_params=small,
            name="project",
        )
        keys_values = project(*xs, wk, wv, *keys_values, *early)
    keys, values = keys_values

    probs, *weights = pl.pallas_call(
        probs_kernel,
        grid=(pairs, MICRO),
        in_specs=[
            pl.BlockSpec((m, PAIR), lambda p, i: (i, p)),
            pl.BlockSpec((enc, PAIR), lambda p, i: (0, p)),
            pl.BlockSpec((1, 2 * m, 1), lambda p, i: (i, 0, 0)),
            pl.BlockSpec((1, enc), lambda p, i: (0, 0)),
            any_spec,
            any_spec,
        ],
        out_specs=[resident] * 3,
        out_shape=[
            in_vmem((MICRO, pairs, 2 * m, enc)),
            in_vmem(wo.shape),
            in_vmem(wq.shape),
        ],
        scratch_shapes=[pltpu.SemaphoreType.DMA((2,))],
        compiler_params=small,
        name="probs",
    )(queries, keys, token_ids, key_ids, in_hbm(wo), in_hbm(wq))


    def turn(t, ups, held, after):
        if parts == 1:
            ups = [jnp.concatenate(ups, axis=0)] if n > 1 else ups
        return pl.pallas_call(
            functools.partial(turn_kernel, parts, r, t, block),
            grid_spec=pltpu.PrefetchScalarGridSpec(
                num_scalar_prefetch=1,
                grid=(width // block,),
                in_specs=[resident] * (parts + 5 + len(held)) + [any_spec] * len(after),
                out_specs=[resident] * 4,
                scratch_shapes=[pltpu.VMEM((m, model), f32)],
            ),
            out_shape=[
                in_vmem((r, model)),
                in_vmem((m - r, model)),
                in_vmem((MICRO + 1, pairs, 2 * m, enc)),
                in_vmem((MICRO + 1, m, width)),
            ],
            input_output_aliases={parts + 6 + i: 2 + i for i in range(len(held))},
            compiler_params=least,
            name="turn",
        )(slots, *ups, *weights, keys, values, probs, *held, *after)

    def norm_back(t, got, own_part, up_own, held):
        k = len(got)
        return pl.pallas_call(
            functools.partial(norm_kernel, k, t),
            grid_spec=pltpu.PrefetchScalarGridSpec(
                num_scalar_prefetch=1,
                grid=(1,),
                in_specs=[resident] * (k + 4 + len(held)),
                out_specs=[resident] * 2,
            ),
            out_shape=[in_vmem((r, model)), in_vmem(((MICRO + 1) * r, model))],
            input_output_aliases={k + 5: 1} if held else {},
            compiler_params=least,
            name="norm",
        )(slots, *got, own_part, up_own, x_own, gain, *held)

    held, dec_held = [], []
    hops = {}
    for t in range(turns):
        if t < MICRO:
            up_own = cotangent[0, t * r : (t + 1) * r]
            if t >= SKEW:
                up_own, _ = lax.optimization_barrier((up_own, own_part))
                up_own = jnp.where(is_last, up_own, hops[t - SKEW])
        else:
            up_own = hops[t - SKEW]
        ups = all_parts(up_own)
        own_part, other, *held = turn(t, ups, held, dec_held)
        got = [
            shifted(other if n == 2 else other[(k - 1) * r : k * r], -k) for k in range(1, n)
        ]
        mine, *dec_held = norm_back(t, got, own_part, up_own, dec_held)
        if t + SKEW < turns:
            hops[t] = along(mine, (3, 2), (2, 1), (1, 0))

    kg, vg = pl.pallas_call(
        functools.partial(grads_kernel, MICRO),
        grid=(pairs,),
        in_specs=[
            resident,
            resident,
            pl.BlockSpec((tokens, PAIR), lambda p: (0, p)),
            resident,
        ],
        out_specs=[pl.BlockSpec((enc, PAIR), lambda p: (0, p))] * 2,
        out_shape=[jax.ShapeDtypeStruct((enc, width), bf16)] * 2,
        compiler_params=small,
        name="grads",
    )(held[0], probs, in_hbm(queries), held[1])

    out_block = min(OUT_BLOCK, model)

    def back(slot):
        outs = back_call(slot)
        swapped = []
        for i in range(PIECES):
            swapped.append([shifted(outs[k * PIECES + i], -k) for k in range(1, n)])
        return list(zip(outs[:PIECES], swapped))

    def total(parts):
        out, got = parts
        out = out.astype(f32)
        for g in got:
            out = out + g.astype(f32)
        return out

    def behind(x, y):
        return lax.optimization_barrier((x, y))[0]

    def back_call(slot):
        return pl.pallas_call(
            back_kernel,
            grid=(model // out_block,),
            in_specs=[pl.BlockSpec((rows, width), lambda i: (slot, 0))] * 2
            + [pl.BlockSpec((out_block, width), lambda i: (i, 0))] * 2,
            out_specs=[pl.BlockSpec((size, out_block), lambda i: (0, i))] * (n * PIECES),
            out_shape=[jax.ShapeDtypeStruct((size, model), bf16)] * (n * PIECES),
            compiler_params=small,
            name="back",
        )(kg, vg, in_hbm(w_key[0]), in_hbm(w_value[0]))

    far, mid = back(3), back(2)
    got = []
    for i in range(PIECES):
        v = far[i] if i == 0 else behind(far[i], v)
        v = total(v).astype(bf16)
        got.append(along(v, (0, 1), (3, 2)))
    near = back(1)
    up2, down2 = [], []
    for i in range(PIECES):
        held, came = (mid[i], got[i]) if i == 0 else behind((mid[i], got[i]), v)
        v = (total(held) + came.astype(f32)).astype(bf16)
        up2.append(along(v, (0, 1), (1, 2)))
        down2.append(along(v, (3, 2), (2, 1)))
    here = back(0)
    up3, down3 = [], []
    for i in range(PIECES):
        ends = (far[i], near[i], up2[i], down2[i])
        a, b, u, d = ends if i == 0 else behind(ends, v)
        a, b = total(a), total(b)
        v = (jnp.where(section == 2, a, b) + u.astype(f32)).astype(bf16)
        w = (jnp.where(section == 1, a, b) + d.astype(f32)).astype(bf16)
        up3.append(along(v, (0, 1), (1, 2), (2, 3)))
        down3.append(along(w, (3, 2), (2, 1), (1, 0)))
    enc_share = [
        total(h) + u.astype(f32) + d.astype(f32) for h, u, d in zip(here, up3, down3)
    ]
    enc_share = jnp.concatenate(enc_share, axis=0)
    return dec_held[0][:own][None, None], enc_share[None]


def solution(mesh):
    in_specs = (
        P("dp", ("section", "mp"), None),
        P("dp", None),
        P("dp", None),
        P("dp", None),
        P("dp", "section", "mp", None),
        P("section", None),
        P("section", None, "mp"),
        P("section", None, "mp"),
        P("section", None, "mp"),
        P("section", "mp", None),
        P("dp", "mp", None),
    )
    out_specs = (P("dp", "section", "mp", None), P("dp", ("section", "mp"), None))
    return jax.shard_map(
        all_of_it, mesh=mesh, in_specs=in_specs, out_specs=out_specs, check_vma=False
    )
```

```python
import functools

import jax
import jax.numpy as jnp
from jax import lax
from jax.experimental import pallas as pl
from jax.experimental.pallas import tpu as pltpu
from jax.sharding import PartitionSpec as P

HD = 64
PAIR = 2 * HD
MICRO = 4
SKEW = 2
PIECES = 2
BLOCK = 512
OUT_BLOCK = 512
SLOTS = ((0, 1, 2, 3), (1, 2, 1, 2), (2, 3, 0, 1), (3, 0, 3, 0))

epsilon = 1e-06
masked_value = -1e30
f32 = jnp.float32
bf16 = jnp.bfloat16
NT = (((1,), (1,)), ((), ()))
NN = (((1,), (0,)), ((), ()))


def dot(a, b, dims):
    return lax.dot_general(a, b, dims, preferred_element_type=f32)


def stacked(x):
    lane = lax.broadcasted_iota(jnp.int32, x.shape, 1)
    zero = jnp.zeros_like(x)
    return jnp.concatenate(
        [jnp.where(lane < HD, x, zero), jnp.where(lane >= HD, x, zero)], axis=0
    )


def probs_kernel(q_ref, k_ref, tok_ref, key_ref, wo_ref, wq_ref, p_ref, wo_out, wq_out, sems):
    first = (pl.program_id(0) == 0) & (pl.program_id(1) == 0)
    last = pl.program_id(0) == pl.num_programs(0) - 1
    last = last & (pl.program_id(1) == pl.num_programs(1) - 1)
    copies = [
        pltpu.make_async_copy(wo_ref, wo_out, sems.at[0]),
        pltpu.make_async_copy(wq_ref, wq_out, sems.at[1]),
    ]

    @pl.when(first)
    def _():
        for copy in copies:
            copy.start()

    q = stacked(q_ref[...].astype(f32) * (HD**-0.5)).astype(bf16)
    s = dot(q, k_ref[...], NT)
    s = jnp.where(tok_ref[0] == key_ref[...], s, masked_value)
    e = jnp.exp(s - jnp.max(s, axis=-1, keepdims=True))
    total = jnp.sum(e, axis=-1, keepdims=True)
    p_ref[pl.program_id(1), pl.program_id(0)] = (e * (1.0 / total)).astype(bf16)

    @pl.when(last)
    def _():
        for copy in copies:
            copy.wait()


def project_kernel(count, slot, block, *refs):
    x_refs = refs[:count]
    wk_ref, wv_ref = refs[count : count + 2]
    k_ref, v_ref, x_all = refs[-3:]

    @pl.when(pl.program_id(0) == 0)
    def _():
        start = 0
        for x in x_refs:
            x_all[start : start + x.shape[0]] = x[...]
            start += x.shape[0]

    cols = pl.ds(pl.multiple_of(pl.program_id(0) * block, block), block)
    rows = slice(slot * x_all.shape[0], (slot + 1) * x_all.shape[0])
    k_ref[rows, cols] = dot(x_all[...], wk_ref[:, cols], NN).astype(bf16)
    v_ref[rows, cols] = dot(x_all[...], wv_ref[:, cols], NN).astype(bf16)


def back_kernel(kg_ref, vg_ref, wk_ref, wv_ref, *out_refs):
    block = out_refs[0].shape[1]
    place = pl.ds(pl.multiple_of(pl.program_id(0) * block, block), block)
    out = dot(kg_ref[...], wk_ref[place, :], NT) + dot(vg_ref[...], wv_ref[place, :], NT)
    rows = out_refs[0].shape[0]
    for i, ref in enumerate(out_refs):
        ref[...] = out[i * rows : (i + 1) * rows].astype(bf16)


def turn_kernel(parts, own_rows, t, block, slots, *refs):
    read, write = slots[t, 0], slots[t, 1]
    up_refs = refs[:parts]
    wo_ref, wq_ref, k_ref, v_ref, p_ref = refs[parts : parts + 5]
    own_ref, other_ref, ds_ref, ag_ref, acc_ref = refs[-5:]
    step = pl.program_id(0)
    start = pl.multiple_of(step * block, block)
    up = up_refs[0][...] if parts == 1 else jnp.concatenate([r[...] for r in up_refs], axis=0)
    rows = up.shape[0]
    grads = dot(up, wo_ref[pl.ds(start, block), :], NT).astype(bf16)
    ag_ref[write, :, pl.ds(start, block)] = grads
    wide = grads.astype(f32)
    lane = lax.broadcasted_iota(jnp.int32, (rows, PAIR), 1)
    pieces = []
    for pair in range(grads.shape[1] // PAIR):
        cols = pl.ds(pl.multiple_of(start + pair * PAIR, PAIR), PAIR)
        here = wide[:, pair * PAIR : (pair + 1) * PAIR]
        pg = dot(stacked(here).astype(bf16), v_ref[:, cols], NT)
        place = step * (block // PAIR) + pair
        p = p_ref[read, place].astype(f32)
        mean = jnp.sum(pg * p, axis=-1, keepdims=True)
        ds = (p * (pg - mean)).astype(bf16)
        ds_ref[write, place] = ds
        both = dot(ds, k_ref[:, cols], NN)
        mine = jnp.where(lane < HD, both[:rows], both[rows:]) * (HD**-0.5)
        pieces.append(mine.astype(bf16))
    qg = pieces[0] if len(pieces) == 1 else jnp.concatenate(pieces, axis=1)
    partial = dot(qg, wq_ref[:, pl.ds(start, block)], NT)

    @pl.when(step == 0)
    def _():
        acc_ref[...] = partial

    @pl.when(step > 0)
    def _():
        acc_ref[...] += partial

    @pl.when(step == pl.num_programs(0) - 1)
    def _():
        own_ref[...] = acc_ref[:own_rows].astype(bf16)
        other_ref[...] = acc_ref[own_rows:].astype(bf16)


def norm_kernel(received, t, slots, *refs):
    got_refs = refs[:received]
    own_ref, up_ref, x_ref, gain_ref = refs[received : received + 4]
    mine_ref, all_ref = refs[-2:]
    rows = mine_ref.shape[0]
    x = x_ref[pl.ds(pl.multiple_of(slots[t, 0] * rows, rows), rows), :].astype(f32)
    recip = lax.rsqrt(jnp.mean(x * x, axis=-1, keepdims=True) + epsilon)
    unit = x * recip
    summed = own_ref[...].astype(f32)
    for got in got_refs:
        summed = summed + got[...].astype(f32)
    scaled = summed * gain_ref[...]
    out = up_ref[...].astype(f32) + recip * (
        scaled - unit * jnp.mean(scaled * unit, axis=-1, keepdims=True)
    )
    out = out.astype(bf16)
    mine_ref[...] = out
    all_ref[pl.ds(pl.multiple_of(slots[t, 1] * rows, rows), rows), :] = out


def grads_kernel(
    micro, ds_ref, p_ref, q_ref, ag_ref, wk_ref, wv_ref, kg_ref, vg_ref, wk_out, wv_out, sems
):
    copies = [
        pltpu.make_async_copy(wk_ref, wk_out, sems.at[0]),
        pltpu.make_async_copy(wv_ref, wv_out, sems.at[1]),
    ]

    @pl.when(pl.program_id(0) == 0)
    def _():
        for copy in copies:
            copy.start()

    rows = ag_ref.shape[1]
    pair = pl.program_id(0)
    cols = pl.ds(pl.multiple_of(pair * PAIR, PAIR), PAIR)
    q = jnp.concatenate(
        [stacked(q_ref[i * rows : (i + 1) * rows, :].astype(f32)) for i in range(micro)], axis=0
    )
    ag = jnp.concatenate(
        [stacked(ag_ref[i, :, cols].astype(f32)) for i in range(micro)], axis=0
    )
    ds = jnp.concatenate([ds_ref[i, pair] for i in range(micro)], axis=0)
    p = jnp.concatenate([p_ref[i, pair] for i in range(micro)], axis=0)
    kg = dot(q.T.astype(bf16), ds, NN) * (HD**-0.5)
    vg = dot(ag.T.astype(bf16), p, NN)
    kg_ref[...] = kg.T.astype(bf16)
    vg_ref[...] = vg.T.astype(bf16)

    @pl.when(pl.program_id(0) == pl.num_programs(0) - 1)
    def _():
        for copy in copies:
            copy.wait()


def all_of_it(
    enc_rows,
    pack_index,
    enc_segments,
    dec_segments,
    dec_inputs,
    norm_gain,
    w_query,
    w_key,
    w_value,
    w_out,
    cotangent,
):
    wq, wk, wv, wo = w_query[0], w_key[0], w_value[0], w_out[0]
    gain = norm_gain.astype(f32)
    model, width = wq.shape
    pairs = width // PAIR
    n = lax.axis_size("mp")
    sections = lax.axis_size("section")
    me = lax.axis_index("mp")
    section = lax.axis_index("section")
    assert sections == len(SLOTS)
    share = enc_rows.shape[1]
    enc = share * n * sections
    own = dec_inputs.shape[2]
    r = own // MICRO
    m = r * n
    tokens = own * n
    params = pltpu.CompilerParams(vmem_limit_bytes=24 * 1024 * 1024)
    small = pltpu.CompilerParams(vmem_limit_bytes=10 * 1024 * 1024)
    least = pltpu.CompilerParams(vmem_limit_bytes=5 * 1024 * 1024)

    def shifted(x, by):
        return lax.ppermute(x, "mp", [((i + by) % n, i) for i in range(n)])

    def along(x, *pairs):
        return lax.ppermute(x, "section", pairs)

    low = section < 2
    block = min(BLOCK, width)
    parts = 2 if n == 2 else 1
    any_spec = pl.BlockSpec(memory_space=pl.ANY)
    resident = pl.BlockSpec(memory_space=pltpu.MemorySpace.VMEM)

    def in_hbm(x):
        return pltpu.with_memory_space_constraint(x, pltpu.MemorySpace.HBM)

    def in_vmem(shape):
        return pltpu.MemorySpace.VMEM(shape, bf16)

    def all_parts(x):
        return [x] + [shifted(x, k) for k in range(1, n)]

    x_own = dec_inputs[0, 0]
    x_all = jnp.stack([v.reshape(MICRO, r, model) for v in all_parts(x_own)], axis=1)
    x_all = x_all.reshape(tokens, model).astype(f32)
    recip = lax.rsqrt(jnp.mean(x_all * x_all, axis=-1, keepdims=True) + epsilon)
    normed = (x_all * recip * gain).astype(bf16)
    queries = dot(normed, wq, NN).astype(bf16)
    token_ids = dec_segments[0].reshape(n, MICRO, r)
    order = jnp.remainder(me + jnp.arange(n), n)
    token_ids = jnp.take(token_ids, order, axis=0).transpose(1, 0, 2).reshape(MICRO, m)
    token_ids = jnp.concatenate([token_ids, token_ids], axis=1)[:, :, None]

    blocks = jnp.asarray(SLOTS, jnp.int32)[:, section]
    stored = (blocks[:, None] * n + order[None, :])[:, :, None] * share
    stored = (stored + jnp.arange(share)).reshape(1, enc)
    key_ids = jnp.sum(
        jnp.where(pack_index[0][:, None] == stored, enc_segments[0][:, None], 0),
        axis=0,
        keepdims=True,
    )
    turns = MICRO + SKEW * (sections - 1)
    micro = jnp.arange(turns, dtype=jnp.int32) - SKEW * (sections - 1 - section)
    read = jnp.clip(micro, 0, MICRO - 1)
    slots = jnp.stack([read, jnp.where(micro == read, read, MICRO)], axis=1)
    outer = (section == 0) | (section == 3)
    is_last = section == sections - 1
    is_first, is_second = section == 1, section == 2
    wk, wv, low, outer, is_last, is_first, is_second, slots = lax.optimization_barrier(
        (wk, wv, low, outer, is_last, is_first, is_second, slots)
    )
    size = share // PIECES
    mine = [enc_rows[0, i * size : (i + 1) * size] for i in range(PIECES)]

    def ring(values, *pairs):
        out = []
        for v in values:
            out.append(along(v, *pairs))
        return out

    up1 = ring(mine, (0, 1), (1, 2), (2, 3))
    down1 = ring(mine, (3, 2), (2, 1), (1, 0))
    up2 = ring(up1, (1, 2), (2, 3))
    down2 = ring(down1, (2, 1), (1, 0))
    third = [jnp.where(low, d, u) for u, d in zip(up2, down2)]
    third = ring(third, (2, 3), (1, 0))
    near_in = [jnp.where(low, d, u) for u, d in zip(up1, down1)]
    far_in = lax.optimization_barrier([jnp.where(low, u, d) for u, d in zip(up1, down1)])
    mid_in = [jnp.where(low, d, u) for u, d in zip(up2, down2)]
    last_in = [jnp.where(outer, t, f) for t, f in zip(third, far_in)]
    slots_in = [mine, near_in, mid_in, last_in]
    keys_values = []
    rows = share * n
    for slot, held in enumerate(slots_in):
        xs = [all_parts(v) for v in held]
        xs = [x[k] for k in range(n) for x in xs]
        early = [] if slot else [slots, key_ids, token_ids]
        if n > 2:
            xs = [jnp.concatenate(xs, axis=0)]
        project = pl.pallas_call(
            functools.partial(project_kernel, len(xs), slot, block),
            grid=(width // block,),
            in_specs=[pl.BlockSpec(x.shape, lambda i: (0, 0)) for x in xs]
            + [resident] * (2 + len(keys_values))
            + [any_spec] * len(early),
            out_specs=[resident] * 2,
            out_shape=[in_vmem((enc, width))] * 2,
            scratch_shapes=[pltpu.VMEM((rows, model), bf16)],
            input_output_aliases={len(xs) + 2 + i: i for i in range(len(keys_values))},
            compiler_params=small,
            name="project",
        )
        keys_values = project(*xs, wk, wv, *keys_values, *early)
    keys, values = keys_values

    probs, *weights = pl.pallas_call(
        probs_kernel,
        grid=(pairs, MICRO),
        in_specs=[
            pl.BlockSpec((m, PAIR), lambda p, i: (i, p)),
            pl.BlockSpec((enc, PAIR), lambda p, i: (0, p)),
            pl.BlockSpec((1, 2 * m, 1), lambda p, i: (i, 0, 0)),
            pl.BlockSpec((1, enc), lambda p, i: (0, 0)),
            any_spec,
            any_spec,
        ],
        out_specs=[resident] * 3,
        out_shape=[
            in_vmem((MICRO, pairs, 2 * m, enc)),
            in_vmem(wo.shape),
            in_vmem(wq.shape),
        ],
        scratch_shapes=[pltpu.SemaphoreType.DMA((2,))],
        compiler_params=small,
        name="probs",
    )(queries, keys, token_ids, key_ids, in_hbm(wo), in_hbm(wq))


    def turn(t, ups, held, after):
        if parts == 1:
            ups = [jnp.concatenate(ups, axis=0)] if n > 1 else ups
        return pl.pallas_call(
            functools.partial(turn_kernel, parts, r, t, block),
            grid_spec=pltpu.PrefetchScalarGridSpec(
                num_scalar_prefetch=1,
                grid=(width // block,),
                in_specs=[resident] * (parts + 5 + len(held)) + [any_spec] * len(after),
                out_specs=[resident] * 4,
                scratch_shapes=[pltpu.VMEM((m, model), f32)],
            ),
            out_shape=[
                in_vmem((r, model)),
                in_vmem((m - r, model)),
                in_vmem((MICRO + 1, pairs, 2 * m, enc)),
                in_vmem((MICRO + 1, m, width)),
            ],
            input_output_aliases={parts + 6 + i: 2 + i for i in range(len(held))},
            compiler_params=least,
            name="turn",
        )(slots, *ups, *weights, keys, values, probs, *held, *after)

    def norm_back(t, got, own_part, up_own, held):
        k = len(got)
        return pl.pallas_call(
            functools.partial(norm_kernel, k, t),
            grid_spec=pltpu.PrefetchScalarGridSpec(
                num_scalar_prefetch=1,
                grid=(1,),
                in_specs=[resident] * (k + 4 + len(held)),
                out_specs=[resident] * 2,
            ),
            out_shape=[in_vmem((r, model)), in_vmem(((MICRO + 1) * r, model))],
            input_output_aliases={k + 5: 1} if held else {},
            compiler_params=least,
            name="norm",
        )(slots, *got, own_part, up_own, x_own, gain, *held)

    held, dec_held = [], []
    hops = {}
    for t in range(turns):
        if t < MICRO:
            up_own = cotangent[0, t * r : (t + 1) * r]
            if t >= SKEW:
                up_own, _ = lax.optimization_barrier((up_own, own_part))
                up_own = jnp.where(is_last, up_own, hops[t - SKEW])
        else:
            up_own = hops[t - SKEW]
        ups = all_parts(up_own)
        own_part, other, *held = turn(t, ups, held, dec_held)
        got = [
            shifted(other if n == 2 else other[(k - 1) * r : k * r], -k) for k in range(1, n)
        ]
        mine, *dec_held = norm_back(t, got, own_part, up_own, dec_held)
        if t + SKEW < turns:
            hops[t] = along(mine, (3, 2), (2, 1), (1, 0))

    kg, vg, wk_back, wv_back = pl.pallas_call(
        functools.partial(grads_kernel, MICRO),
        grid=(pairs,),
        in_specs=[
            resident,
            resident,
            pl.BlockSpec((tokens, PAIR), lambda p: (0, p)),
            resident,
            any_spec,
            any_spec,
        ],
        out_specs=[pl.BlockSpec((enc, PAIR), lambda p: (0, p))] * 2 + [resident] * 2,
        out_shape=[jax.ShapeDtypeStruct((enc, width), bf16)] * 2
        + [in_vmem(wk.shape), in_vmem(wv.shape)],
        scratch_shapes=[pltpu.SemaphoreType.DMA((2,))],
        compiler_params=least,
        name="grads",
    )(
        held[0], probs, in_hbm(queries), held[1], in_hbm(w_key[0]), in_hbm(w_value[0])
    )

    out_block = min(OUT_BLOCK, model)

    def back(slot):
        outs = back_call(slot)
        swapped = []
        for i in range(PIECES):
            swapped.append([shifted(outs[k * PIECES + i], -k) for k in range(1, n)])
        return list(zip(outs[:PIECES], swapped))

    def total(parts):
        out, got = parts
        out = out.astype(f32)
        for g in got:
            out = out + g.astype(f32)
        return out

    def behind(x, y):
        return lax.optimization_barrier((x, y))[0]

    def back_call(slot):
        return pl.pallas_call(
            back_kernel,
            grid=(model // out_block,),
            in_specs=[pl.BlockSpec((rows, width), lambda i: (slot, 0))] * 2
            + [resident] * 2,
            out_specs=[pl.BlockSpec((size, out_block), lambda i: (0, i))] * (n * PIECES),
            out_shape=[jax.ShapeDtypeStruct((size, model), bf16)] * (n * PIECES),
            compiler_params=least,
            name="back",
        )(kg, vg, wk_back, wv_back)

    far, mid = back(3), back(2)
    got = []
    for i in range(PIECES):
        v = far[i] if i == 0 else behind(far[i], v)
        v = total(v).astype(bf16)
        got.append(along(v, (0, 1), (3, 2)))
    near = back(1)
    up2, down2 = [], []
    for i in range(PIECES):
        held, came = (mid[i], got[i]) if i == 0 else behind((mid[i], got[i]), v)
        v = (total(held) + came.astype(f32)).astype(bf16)
        up2.append(along(v, (0, 1), (1, 2)))
        down2.append(along(v, (3, 2), (2, 1)))
    here = back(0)
    up3, down3 = [], []
    for i in range(PIECES):
        ends = (far[i], near[i], up2[i], down2[i])
        a, b, u, d = ends if i == 0 else behind(ends, v)
        a, b = total(a), total(b)
        v = (jnp.where(is_second, a, b) + u.astype(f32)).astype(bf16)
        w = (jnp.where(is_first, a, b) + d.astype(f32)).astype(bf16)
        up3.append(along(v, (0, 1), (1, 2), (2, 3)))
        down3.append(along(w, (3, 2), (2, 1), (1, 0)))
    enc_share = [
        total(h) + u.astype(f32) + d.astype(f32) for h, u, d in zip(here, up3, down3)
    ]
    enc_share = jnp.concatenate(enc_share, axis=0)
    return dec_held[0][:own][None, None], enc_share[None]


def solution(mesh):
    in_specs = (
        P("dp", ("section", "mp"), None),
        P("dp", None),
        P("dp", None),
        P("dp", None),
        P("dp", "section", "mp", None),
        P("section", None),
        P("section", None, "mp"),
        P("section", None, "mp"),
        P("section", None, "mp"),
        P("section", "mp", None),
        P("dp", "mp", None),
    )
    out_specs = (P("dp", "section", "mp", None), P("dp", ("section", "mp"), None))
    return jax.shard_map(
        all_of_it, mesh=mesh, in_specs=in_specs, out_specs=out_specs, check_vma=False
    )
```
